32 devices in a mesh: dp: 8 (over z, x), expert: 4 (over y, core).
Axes of the slice: x: 2, y: 2, z: 4, core: 2. Of those that a mesh axis runs over, the one named last changes fastest.
Arguments:
- tokens: bfloat16 [8192, 768], P(('dp', 'expert')), may hold values from -6 to 6
- expert_ids: int32 [8192, 2], P(('dp', 'expert')), may hold values from 0 to 15, all different within a row; in each aligned block of 256 rows (0 to 255, 256 to 511, ...) at most 64 rows name the same one
- gate_fixed: int32 [8192, 2], P(('dp', 'expert')), may hold values from 8192 to 65535
- cotangent: bfloat16 [8192, 768], P(('dp', 'expert')), may hold values from -6 to 6
- w_gate: bfloat16 [16, 768, 384], P('expert'), may hold values from -0.21875 to 0.21875
- w_up: bfloat16 [16, 768, 384], P('expert'), may hold values from -0.21875 to 0.21875
- w_down: bfloat16 [16, 768, 384], P('expert'), may hold values from -0.3125 to 0.3125
Outputs:
- layer_out: bfloat16 [8192, 768], P(('dp', 'expert'))
- input_grad: bfloat16 [8192, 768], P(('dp', 'expert'))
- grad_gate: float32 [16, 768, 384], P('expert', 'dp')
- grad_up: float32 [16, 768, 384], P('expert', 'dp')
- grad_down: float32 [16, 768, 384], P('expert', 'dp')
The draws below stay inside these ranges and needn't reach their ends.
Inputs may be any that keep to these rules, and one draw needn't show every extreme that they name: `expert_ids`: A row names 2 different experts. In each aligned block of 256 rows (the rows of one device) no expert is named by more than 64 rows, and in some block one expert is named by exactly 64 rows.
All inputs are finite; a program needn't handle non-finite values.
Results may differ from the reference program's by a relative error of at most 0.015.
Values may be sent and summed in bfloat16 or wider, within the bound.
A program may use at most 64 MiB of HBM per device.

```python
import math
import jax
import jax.numpy as jnp
import numpy as np
from jax import lax

D = 768
FF = 384
TOP = 2
TOK_DEV = 256
EXPERTS = 16
TOKENS = 8192
CAP = 64
LOAD = 1024


def plant(result, stream_key, low, largest):
    index_at = [jax.random.randint(jax.random.fold_in(stream_key, axis), (), 0, length) for axis, length in enumerate(result.shape)]
    widest = result.shape.index(max(result.shape))
    neighbour = index_at[:widest] + [(index_at[widest] + 1) % result.shape[widest]] + index_at[widest + 1:]
    return result.at[tuple(index_at)].set(low).at[tuple(neighbour)].set(largest)


def raised(drawn, stream_key, source, target, parts, factor):
    owner, partner = [(jnp.arange(drawn.shape[dim]) // (drawn.shape[dim] // parts)).reshape([-1 if axis == dim else 1 for axis in range(drawn.ndim)]) for dim in (source, target)]
    chosen = jax.random.permutation(stream_key, parts)[partner]
    strong = (owner == chosen) | (owner == (partner + parts // 2) % parts)
    return jnp.where(strong, factor * drawn, drawn)


def shard_levels(rng, shape, split, least, top_value):
    loudness, own = 1.0, jax.random.fold_in(rng, 6)
    for dim, shards_of in split:
        steps = jnp.exp(jax.random.uniform(jax.random.fold_in(own, dim), (shards_of,), jnp.float32, least / len(split), top_value / len(split)))
        loudness = loudness * jnp.repeat(steps, shape[dim] // shards_of).reshape([-1 if axis == dim else 1 for axis in range(len(shape))])
    return loudness


def routed_block(key, own, number, rows, amount, top, most, skew):
    ranking = jax.random.permutation(key, amount)
    packed, ordinary = load_shares(amount, rows * top, most, skew, True), load_shares(amount, rows * top, most, skew, False)
    places = jnp.arange(amount)

    def named(lengths, rotation):
        used = int((lengths > 0).sum())
        fixed = max(1, used // 4)
        moved = fixed + (places - fixed + rotation * (used - fixed)) % max(1, amount - fixed)
        return jnp.zeros((amount,), jnp.int32).at[ranking[jnp.where(places < fixed, places, moved)]].set(jnp.asarray(lengths, jnp.int32))

    lengths = jnp.where(number % 4 == 0, named(packed, number // 4), named(ordinary, number - number // 4 - 1))
    mixed = jax.random.permutation(jax.random.fold_in(own, 3), amount)
    donor, receiver = mixed[0:amount // 2 * 2:2], mixed[1:amount // 2 * 2:2]
    margin = jnp.minimum(lengths[donor] - 1, most - lengths[receiver]) // 2
    margin = jnp.where((donor == ranking[0]) | (receiver == ranking[0]) | (lengths[receiver] == 0), 0, jnp.maximum(margin, 0))
    moved = jax.random.randint(jax.random.fold_in(own, 4), (amount // 2,), 0, 1 << 20) % (margin + 1)
    lengths = lengths.at[donor].add(-moved).at[receiver].add(moved)
    items = jnp.searchsorted(jnp.cumsum(lengths), jnp.arange(rows * top), side="right").astype(jnp.int32)
    table = items.reshape(top, rows).T
    table = table[jax.random.permutation(jax.random.fold_in(own, 1), rows)]
    rotation = jax.random.randint(jax.random.fold_in(own, 2), (rows, 1), 0, top)
    return jnp.take_along_axis(table, (jnp.arange(top)[None, :] + rotation) % top, axis=1)


def load_shares(count, total, most, skew, full):
    weights = [(1 << 20) // math.isqrt(standing ** skew) + 1 for standing in range(1, count + 1)]
    largest = most if full else min(most, max(-(-total // count), total * weights[0] // sum(weights)))
    least = 1 if total - largest >= count - 1 else 0
    holding, spare = [largest] + [least] * (count - 1), total - largest - least * (count - 1)
    while spare > 0:
        movable = [i for i in range(1, count) if holding[i] < largest] or [i for i in range(1, count) if holding[i] < most]
        whole, budget = sum([weights[i] for i in movable]), spare
        for i in movable:
            more = min(most - holding[i], max(1, budget * weights[i] // whole), spare)
            holding[i] = holding[i] + more
            spare = spare - more
    return np.array(holding)


def bell_draw(rng, shape, width, most, pieces=(), kind=jnp.bfloat16):
    gain = shard_levels(rng, shape, pieces, -0.22, 0.18) if pieces else 1.0
    drawn = jax.random.normal(rng, shape, jnp.float32) * width * gain
    return jnp.minimum(jnp.maximum(drawn, -most), most).astype(kind)


def noise_with(rng, dims, scale, bound, pieces, heavy, kind=jnp.bfloat16):
    values = scale * jax.random.normal(rng, dims, jnp.float32)
    if pieces:
        values = values * shard_levels(rng, dims, pieces, -0.22, 0.18)
    return jnp.clip(raised(values, jax.random.fold_in(rng, 3), *heavy), -bound, bound).astype(kind)


def setup_inputs(seed: int = 0) -> dict:
    key_list = jax.random.split(jax.random.key(seed), 8)
    tokens = noise_with(key_list[0], (TOKENS, D), 1.0, 6.0, ((0, 32),), (0, 1, 32, 2.75))
    expert_ids_keys = jax.random.split(jax.random.fold_in(key_list[1], 1), TOKENS // TOK_DEV)
    expert_ids_turns = jax.random.permutation(jax.random.fold_in(key_list[1], 3), TOKENS // TOK_DEV)
    expert_ids = jax.vmap(lambda own, number: routed_block(jax.random.fold_in(key_list[1], 2), own, number, TOK_DEV, EXPERTS, TOP, CAP, 1))(expert_ids_keys, expert_ids_turns).reshape((TOKENS, TOP))
    gate_fixed = plant(jax.random.randint(key_list[2], (TOKENS, TOP), 8192, 65536), jax.random.fold_in(key_list[2], 1), 8192, 65535).astype(jnp.int32)
    cotangent = noise_with(key_list[3], (TOKENS, D), 1.0, 6.0, ((0, 32),), (0, 1, 32, 2.75))
    w_gate = bell_draw(key_list[4], (EXPERTS, D, FF), D ** -0.5, 0.21875, ((0, 4),))
    w_up = bell_draw(key_list[5], (EXPERTS, D, FF), D ** -0.5, 0.21875, ((0, 4),))
    w_down = bell_draw(key_list[6], (EXPERTS, D, FF), FF ** -0.5, 0.3125, ((0, 4),))
    return {"tokens": tokens, "expert_ids": expert_ids, "gate_fixed": gate_fixed, "cotangent": cotangent, "w_gate": w_gate, "w_up": w_up, "w_down": w_down}


def matmul(left, right):
    return jnp.dot(left.astype(jnp.float32), right.astype(jnp.float32), precision=lax.Precision.HIGHEST)

def reference(tokens, expert_ids, gate_fixed, cotangent, w_gate, w_up, w_down):
    entries = TOKENS * TOP
    flat_ids = expert_ids.reshape(-1).astype(jnp.int32)
    blocks = flat_ids.reshape(-1, TOK_DEV * TOP)
    onehot = (blocks[:, :, None] == jnp.arange(EXPERTS, dtype=jnp.int32)[None, None, :]).astype(jnp.int32)
    slot_rank = lax.optimization_barrier(jnp.sum((jnp.cumsum(onehot, axis=1) - 1) * onehot, axis=2)).reshape(-1)
    block_of = jnp.arange(entries, dtype=jnp.int32) // (TOK_DEV * TOP)
    position = (block_of * CAP + slot_rank).astype(jnp.int32)
    rows_all = TOKENS // TOK_DEV * CAP
    slot_table = jnp.full((EXPERTS, rows_all), entries, jnp.int32)
    slot_table = slot_table.at[flat_ids, position].set(jnp.arange(entries, dtype=jnp.int32))
    gate_values = jnp.concatenate([gate_fixed.reshape(-1).astype(jnp.float32) / 65536.0, jnp.zeros((1,), jnp.float32)])
    grad_scale = 1.0 / math.sqrt(LOAD)

    def one_expert(totals, inputs):
        out_sum, grad_sum = totals
        rows, gate_w, up_w, down_w = inputs
        is_valid = rows < entries
        token_of = jnp.where(is_valid, rows // TOP, 0).astype(jnp.int32)
        rows_in = jnp.where(is_valid[:, None], tokens[token_of], jnp.zeros((), tokens.dtype))
        slot_gate = gate_values[rows]
        grads_in = (slot_gate[:, None] * cotangent[token_of].astype(jnp.float32)).astype(jnp.bfloat16)
        pre_gate = matmul(rows_in, gate_w)
        pre_up = matmul(rows_in, up_w)
        sigmoid_gate = jax.nn.sigmoid(pre_gate)
        activated = pre_gate * sigmoid_gate
        hidden = (activated * pre_up).astype(jnp.bfloat16)
        outputs = matmul(hidden, down_w.T).astype(jnp.bfloat16)
        hidden_grad = matmul(grads_in, down_w)
        gate_grad = (hidden_grad * pre_up * sigmoid_gate * (1.0 + pre_gate * (1.0 - sigmoid_gate))).astype(jnp.bfloat16)
        up_grad = (hidden_grad * activated).astype(jnp.bfloat16)
        entry_grad = (matmul(gate_grad, gate_w.T) + matmul(up_grad, up_w.T)).astype(jnp.bfloat16)
        out_sum = out_sum.at[token_of].add(slot_gate[:, None] * outputs.astype(jnp.float32))
        grad_sum = grad_sum.at[token_of].add(jnp.where(is_valid[:, None], entry_grad.astype(jnp.float32), jnp.zeros((), jnp.float32)))
        weight_gate = matmul(rows_in.T, gate_grad) * grad_scale
        weight_up = matmul(rows_in.T, up_grad) * grad_scale
        weight_down = matmul(grads_in.T, hidden) * grad_scale
        return ((out_sum, grad_sum), (weight_gate, weight_up, weight_down))
    start = (jnp.zeros((TOKENS, D), jnp.float32), jnp.zeros((TOKENS, D), jnp.float32))
    (out_sum, grad_sum), (grad_gate, grad_up, grad_down) = lax.scan(one_expert, start, (slot_table, w_gate, w_up, w_down))
    return (out_sum.astype(jnp.bfloat16), grad_sum.astype(jnp.bfloat16), grad_gate, grad_up, grad_down)
```

```python
import functools

import jax
import jax.numpy as jnp
from jax import lax
from jax.experimental import pallas as pl
from jax.experimental.pallas import tpu as pltpu
from jax.sharding import PartitionSpec as P

BF = jnp.bfloat16
F32 = jnp.float32


def dot(a, b, ca=1, cb=0):
    return lax.dot_general(a, b, (((ca,), (cb,)), ((), ())), preferred_element_type=F32)


def flipped(me, k):
    out, bit = me, 1
    while bit <= k:
        if k & bit:
            out = out + bit * (1 - 2 * lax.rem(lax.div(me, bit), 2))
        bit *= 2
    return out


def kernel(
    n, inner, outer, top,
    ids, gates, tok, cot, wg_h, wu_h, wd_h,
    act_o, grad_o,
    wgu, wd, ids_r, gates_r, rows_r, hot, hot1, slot_gate, slot_gate1,
    xs, gs, xs1, gs1, hs, hs1, pre, gu, gu1, ys, ds, y_r, parts, x_r, z_s, z_r,
    w_sem, ms_sem, mr_sem, gs_sem, gr_sem, ys_sem, yr_sem, xs_sem, xr_sem, zs_sem, zr_sem,
):
    me = lax.axis_index("expert")
    my_dp = lax.axis_index("dp")
    my_z = lax.div(my_dp, inner)
    my_x = lax.rem(my_dp, inner)
    my_zh = lax.div(my_z, 2)
    my_zl = lax.rem(my_z, 2)
    other_x = 1 - my_x
    partner_dp = my_z * inner + other_x
    mate_dp = flipped(my_z, 1) * inner + my_x
    local, d_model, ff2 = wgu.shape
    ff = ff2 // 2
    part = local // 2
    mine = my_zl * part
    tokens = tok.shape[0]
    split = tokens // 2
    cap = slot_gate.shape[2]
    rows = parts.shape[4]
    groups = outer // 2
    own = (tok, cot)

    loads = [
        pltpu.make_async_copy(wg_h, wgu.at[:, :, pl.ds(0, ff)], w_sem.at[0]),
        pltpu.make_async_copy(wu_h, wgu.at[:, :, pl.ds(ff, ff)], w_sem.at[1]),
        pltpu.make_async_copy(wd_h, wd, w_sem.at[2]),
    ]

    barrier = pltpu.get_barrier_semaphore()
    for k in range(1, n):
        pl.semaphore_signal(barrier, inc=1, device_id={"expert": flipped(me, k)})
    for k in range(1, n):
        pl.semaphore_signal(barrier, inc=1, device_id={"dp": mate_dp, "expert": flipped(me, k)})
    pl.semaphore_signal(barrier, inc=1, device_id={"dp": partner_dp})
    for k in range(1, outer):
        pl.semaphore_signal(barrier, inc=1, device_id={"dp": flipped(my_z, k) * inner + my_x})
    pl.semaphore_wait(barrier, 2 * (n - 1) + 1 + (outer - 1))

    def send(src, dst, s, r, **where):
        return pltpu.make_async_remote_copy(src_ref=src, dst_ref=dst, send_sem=s, recv_sem=r, device_id=where)

    def meta_copies(s, k):
        where = {"expert": flipped(me, k)} if k else {}
        if s:
            where["dp"] = mate_dp
        return [
            send(a, b.at[s, k], ms_sem.at[i, s, k], mr_sem.at[i, s, k], **where)
            for i, (a, b) in enumerate(((ids, ids_r), (gates, gates_r)))
        ]

    def row_copies(t, s, k, halves=(0, 1)):
        sems = lambda h: (gs_sem.at[t, s, k, h], gr_sem.at[t, s, k, h])
        landed = rows_r.at[t, s, k]
        if s == 0:
            if k % 2 and k > 1:
                return [send(rows_r.at[t, 0, k - 1], landed, *sems(0), expert=flipped(me, 1))]
            return [send(own[t], landed, *sems(0), expert=flipped(me, k))]
        if k == 0:
            return [send(own[t], landed, *sems(0), dp=mate_dp)]
        if k % 2:
            return [send(rows_r.at[t, 1, k - 1], landed, *sems(0), expert=flipped(me, 1))]
        span = (pl.ds(0, split), pl.ds(split, tokens - split))
        src = (rows_r.at[t, 0, k], rows_r.at[t, 1, 0])
        where = ({"dp": mate_dp}, {"expert": flipped(me, k)})
        return [send(src[h].at[span[h]], landed.at[span[h]], *sems(h), **where[h]) for h in halves]

    def start(copies):
        for c in copies:
            c.start()

    def landed(copies):
        for c in copies:
            c.wait_recv()

    def left(copies):
        for c in copies:
            c.wait_send()

    pairs = [(0, k) for k in range(1, n)] + [(1, k) for k in range(n)]
    for s, k in pairs:
        start(meta_copies(s, k))
    direct = [(0, k) for k in range(2, n, 2)] + [(1, 0), (0, 1)]
    for t in range(2):
        for s, k in direct:
            start(row_copies(t, s, k))
    for c in loads:
        c.start()

    above = (
        lax.broadcasted_iota(jnp.int32, (tokens, tokens), 0)
        < lax.broadcasted_iota(jnp.int32, (tokens, tokens), 1)
    )
    before = jnp.where(above, 1.0, 0.0).astype(BF)
    padded = -(-local // 8) * 8

    def route(s, k):
        if s or k:
            landed(meta_copies(s, k))
            iv, gv = ids_r[s, k], gates_r[s, k]
        else:
            iv, gv = ids[...], gates[...]
        count, first = (part, me * local + mine) if s else (local, me * local)
        hots, values = (hot1, slot_gate1) if s else (hot, slot_gate)
        expert = lax.broadcasted_iota(jnp.int32, (padded, tokens), 0) + first
        hit = jnp.zeros((padded, tokens), F32)
        gate = jnp.zeros((padded, tokens), F32)
        for c in range(top):
            same = iv[c : c + 1] == expert
            hit = hit + jnp.where(same, 1.0, 0.0)
            gate = gate + jnp.where(same, gv[c : c + 1].astype(F32) * (1.0 / 65536.0), 0.0)
        rank = dot(hit.astype(BF), before)
        rank = jnp.where(hit > 0.5, rank, -1.0)
        slot = lax.broadcasted_iota(jnp.int32, (cap, tokens), 0).astype(F32)
        for i in range(count):
            picked = jnp.where(slot == rank[i : i + 1], 1.0, 0.0)
            hots[k, i * cap : (i + 1) * cap] = picked.astype(BF)
            value = jnp.sum(picked * gate[i : i + 1], axis=1, keepdims=True)
            values[k, i] = jnp.broadcast_to(value, (cap, 128))

    def take(t, s, k):
        block = own[t][...] if s == 0 and k == 0 else rows_r[t, s, k]
        got = dot((hot1 if s else hot)[k], block)
        count = part if s else local
        into = ((xs, gs), (xs1, gs1))[s][t]
        for i in range(count):
            value = got[i * cap : (i + 1) * cap]
            if t:
                value = (slot_gate1 if s else slot_gate)[k, i][:, :1] * value
            into[i, k * cap : (k + 1) * cap] = value.astype(BF)

    def x_copy(i, a, j):
        zz = pl.ds(2 * flipped(my_zh, j), 2)
        return send(
            parts.at[other_x, i, a, zz], x_r.at[i, a, zz], xs_sem.at[i, a, j], xr_sem.at[i, a, j], dp=partner_dp
        )

    def z_copy(k, i, a):
        there = flipped(my_z, k)
        return send(
            z_s.at[i, a, there], z_r.at[k, i, a], zs_sem.at[k, i, a], zr_sem.at[k, i, a],
            dp=there * inner + my_x,
        )

    def put(i, a, value):
        for zz in range(outer):
            for xx in range(inner):
                at = (zz * inner + xx) * rows
                parts[xx, i, a, zz] = value[at : at + rows].astype(BF)
        for j in range(groups - 1, 0, -1):
            x_copy(i, a, j).start()

    def grads(hidden_grad, p, into, e):
        pre_gate, pre_up = p[:, :ff], p[:, ff:]
        sig = jax.nn.sigmoid(pre_gate)
        into[e, :, ff:] = (hidden_grad * (pre_gate * sig)).astype(BF)
        into[e, :, :ff] = (hidden_grad * pre_up * sig * (1.0 + pre_gate * (1.0 - sig))).astype(BF)

    def forward(e, carry):
        p = dot(xs[e], wgu[e])
        pre[e] = p
        pre_gate, pre_up = p[:, :ff], p[:, ff:]
        hidden = (pre_gate * jax.nn.sigmoid(pre_gate) * pre_up).astype(BF)
        hs[e] = hidden
        o = dot(hidden, wd[e], 1, 1).astype(BF).astype(F32)
        for k in range(n):
            ys[k, e] = (slot_gate[k, e][:, :1] * o[k * cap : (k + 1) * cap]).astype(BF)
        return carry

    def backward(e, carry):
        grads(dot(gs[e], wd[e]), pre[e], gu, e)
        back = dot(gu[e], wgu[e], 1, 1).astype(BF)
        for k in range(n):
            ds[k, e] = back[k * cap : (k + 1) * cap]
        return carry

    def forward_pair(i, carry):
        p = dot(xs1[i], wgu[mine + i])
        pre[i] = p
        pre_gate, pre_up = p[:, :ff], p[:, ff:]
        hs1[i] = (pre_gate * jax.nn.sigmoid(pre_gate) * pre_up).astype(BF)
        return carry

    def backward_pair(i, carry):
        e = mine + i
        put(i, 2, dot(gs[e], hs[e], 0, 0) + dot(gs1[i], hs1[i], 0, 0))
        grads(dot(gs1[i], wd[e]), pre[i], gu1, i)
        both = dot(xs[e], gu[e], 0, 0) + dot(xs1[i], gu1[i], 0, 0)
        put(i, 0, both[:, :ff])
        put(i, 1, both[:, ff:])
        return carry

    def y_copy(j, k):
        return send(rows_r.at[j, 0, k], y_r.at[j, k], ys_sem.at[j, k], yr_sem.at[j, k], expert=flipped(me, k))

    def spread(j, k):
        src = (ys, ds)[j]
        return dot(hot[k], src[k].reshape(local * cap, d_model), 0, 0)

    def back_out(j):
        for k in range(n - 1, 0, -1):
            if k % 2 == 0:
                left(row_copies(j, 0, k + 1) + row_copies(j, 1, k, (0,)))
            rows_r[j, 0, k] = spread(j, k).astype(BF)
            y_copy(j, k).start()

    def returned(j):
        total = spread(j, 0)
        for k in range(1, n):
            y_copy(j, k).wait_recv()
            total = total + y_r[j, k].astype(F32)
        act_o[j] = total.astype(BF)

    even = range(2, n, 2)

    def relay(t):
        for k in even:
            landed(row_copies(t, 0, k))
            start(row_copies(t, 0, k + 1))
            start(row_copies(t, 1, k, (0,)))
        landed(row_copies(t, 1, 0))
        for k in even:
            start(row_copies(t, 1, k, (1,)))
        start(row_copies(t, 1, 1))
        for k in even:
            take(t, 0, k)
        take(t, 1, 0)
        for k in even:
            landed(row_copies(t, 0, k + 1))
            take(t, 0, k + 1)
        landed(row_copies(t, 1, 1))
        take(t, 1, 1)

    def relay_far(t):
        for k in even:
            landed(row_copies(t, 1, k))
            start(row_copies(t, 1, k + 1))
            take(t, 1, k)
        for k in even:
            landed(row_copies(t, 1, k + 1))
            take(t, 1, k + 1)

    route(0, 0)
    for t in range(2):
        take(t, 0, 0)
    for s, k in pairs:
        route(s, k)
    for t in range(2):
        landed(row_copies(t, 0, 1))
        take(t, 0, 1)
    relay(0)
    for c in loads:
        c.wait()
    lax.fori_loop(0, local, forward, 0)
    relay(1)
    lax.fori_loop(0, local, backward, 0)
    relay_far(0)
    lax.fori_loop(0, part, forward_pair, 0)
    back_out(0)
    relay_far(1)
    lax.fori_loop(0, part, backward_pair, 0)

    def near(i, carry):
        for a in (2, 0, 1):
            x_copy(i, a, 0).start()
        return carry

    lax.fori_loop(0, part, near, 0)
    back_out(1)

    def x_stage(j):
        def stage(i, carry):
            for a in (2, 0, 1):
                x_copy(i, a, j).wait_recv()
                for low in range(2):
                    zz = 2 * flipped(my_zh, j) + low
                    z_s[i, a, zz] = (parts[my_x, i, a, zz].astype(F32) + x_r[i, a, zz].astype(F32)).astype(BF)
                for low in range(2):
                    if 2 * j + low:
                        z_copy(2 * j + low, i, a).start()
            return carry

        return stage

    for j in range(groups - 1, 0, -1):
        lax.fori_loop(0, part, x_stage(j), 0)
    returned(0)
    lax.fori_loop(0, part, x_stage(0), 0)
    returned(1)

    def finish(i, carry):
        for a in (2, 0, 1):
            total = z_s[i, a, my_z].astype(F32)
            for k in range(2, outer, 2):
                z_copy(k, i, a).wait_recv()
                total = total + z_r[k, i, a].astype(F32)
            grad_o[a, mine + i] = total
            z_copy(1, i, a).wait_recv()
            total = z_r[1, i, a].astype(F32)
            for k in range(3, outer, 2):
                z_copy(k, i, a).wait_recv()
                total = total + z_r[k, i, a].astype(F32)
            grad_o[a, part - mine + i] = total
        return carry

    lax.fori_loop(0, part, finish, 0)

    for s, k in pairs:
        left(meta_copies(s, k))
        for t in range(2):
            if s or k < 2 or k % 2 == 0:
                left(row_copies(t, s, k, (1,)))
    for j in range(2):
        for k in range(1, n):
            y_copy(j, k).wait_send()

    def drain(i, carry):
        for a in range(3):
            for j in range(groups):
                x_copy(i, a, j).wait_send()
            for k in range(1, outer):
                z_copy(k, i, a).wait_send()
        return carry

    lax.fori_loop(0, part, drain, 0)


def write(scale, act, grad, out_o, din_o, gg_o, gu_o, gd_o):
    out_o[...] = act[0]
    din_o[...] = act[1]
    for a, o in enumerate((gg_o, gu_o, gd_o)):
        o[...] = grad[a] * scale


def shards(tokens, expert_ids, gate_fixed, cotangent, w_gate, w_up, w_down):
    n = lax.axis_size("expert")
    replicas = lax.axis_size("dp")
    inner = 2
    outer = replicas // inner
    local, d_model, ff = w_gate.shape
    count, top = expert_ids.shape
    cap = count * top * 2 // (local * n)
    rows = d_model // replicas
    part = local // 2
    scale = float(count * n * replicas * top // (local * n)) ** (-0.5)
    vmem = pl.BlockSpec(memory_space=pltpu.VMEM)
    hbm = pl.BlockSpec(memory_space=pl.ANY)
    dma = pltpu.SemaphoreType.DMA
    slots = n * cap
    act, grad = pl.pallas_call(
        functools.partial(kernel, n, inner, outer, top),
        out_shape=(
            jax.ShapeDtypeStruct((2, count, d_model), BF),
            jax.ShapeDtypeStruct((3, local, rows, ff), F32),
        ),
        in_specs=[vmem] * 4 + [hbm] * 3,
        out_specs=(vmem,) * 2,
        scratch_shapes=[
            pltpu.VMEM((local, d_model, 2 * ff), BF),
            pltpu.VMEM((local, d_model, ff), BF),
            pltpu.VMEM((2, n, top, count), jnp.int32),
            pltpu.VMEM((2, n, top, count), jnp.int32),
            pltpu.VMEM((2, 2, n, count, d_model), BF),
            pltpu.VMEM((n, local * cap, count), BF),
            pltpu.VMEM((n, part * cap, count), BF),
            pltpu.VMEM((n, local, cap, 128), F32),
            pltpu.VMEM((n, part, cap, 128), F32),
            pltpu.VMEM((local, slots, d_model), BF),
            pltpu.VMEM((local, slots, d_model), BF),
            pltpu.VMEM((part, slots, d_model), BF),
            pltpu.VMEM((part, slots, d_model), BF),
            pltpu.VMEM((local, slots, ff), BF),
            pltpu.VMEM((part, slots, ff), BF),
            pltpu.VMEM((local, slots, 2 * ff), F32),
            pltpu.VMEM((local, slots, 2 * ff), BF),
            pltpu.VMEM((part, slots, 2 * ff), BF),
            pltpu.VMEM((n, local, cap, d_model), BF),
            pltpu.VMEM((n, local, cap, d_model), BF),
            pltpu.VMEM((2, n, count, d_model), BF),
            pltpu.VMEM((inner, part, 3, outer, rows, ff), BF),
            pltpu.VMEM((part, 3, outer, rows, ff), BF),
            pltpu.VMEM((part, 3, outer, rows, ff), BF),
            pltpu.VMEM((outer, part, 3, rows, ff), BF),
            dma((3,)),
            dma((2, 2, n)), dma((2, 2, n)),
            dma((2, 2, n, 2)), dma((2, 2, n, 2)),
            dma((2, n)), dma((2, n)),
            dma((part, 3, outer // 2)), dma((part, 3, outer // 2)),
            dma((outer, part, 3)), dma((outer, part, 3)),
        ],
        compiler_params=pltpu.CompilerParams(
            collective_id=0, has_side_effects=True, vmem_limit_bytes=60 * 1024 * 1024
        ),
    )(expert_ids.T, gate_fixed.T, tokens, cotangent, w_gate, w_up, w_down)
    act_block = jax.ShapeDtypeStruct((count, d_model), BF)
    grad_block = jax.ShapeDtypeStruct((local, rows, ff), F32)
    return pl.pallas_call(
        functools.partial(write, scale),
        out_shape=(act_block, act_block, grad_block, grad_block, grad_block),
        in_specs=[vmem] * 2,
        out_specs=(vmem,) * 5,
    )(act, grad)


def solution(mesh):
    return jax.shard_map(
        shards,
        mesh=mesh,
        in_specs=(P(("dp", "expert"), None),) * 4 + (P("expert", None, None),) * 3,
        out_specs=(P(("dp", "expert"), None),) * 2 + (P("expert", "dp", None),) * 3,
        check_vma=False,
    )
```

```python
import functools

import jax
import jax.numpy as jnp
from jax import lax
from jax.experimental import pallas as pl
from jax.experimental.pallas import tpu as pltpu
from jax.sharding import PartitionSpec as P

BF = jnp.bfloat16
F32 = jnp.float32
MARGIN = 6 * 1024 * 1024


def dot(a, b, ca=1, cb=0):
    return lax.dot_general(a, b, (((ca,), (cb,)), ((), ())), preferred_element_type=F32)


def flipped(me, k):
    out, bit = me, 1
    while bit <= k:
        if k & bit:
            out = out + bit * (1 - 2 * lax.rem(lax.div(me, bit), 2))
        bit *= 2
    return out


def kernel(
    n, inner, outer, top, scale,
    ids_h, gates_h, tok_h, cot_h, wg_h, wu_h, wd_h,
    act_o, grad_o,
    act_s, grad_s, wgu, wd, ids_r, gates_r, rows_r, hot, hot1, slot_gate, slot_gate1,
    xs, gs, xs1, gs1, hs, hs1, pre, gu, gu1, ys, ds, y_r, parts, x_r, z_s, z_r,
    w_sem, in_sem, out_sem, ms_sem, mr_sem, gs_sem, gr_sem, ys_sem, yr_sem, xs_sem, xr_sem, zs_sem, zr_sem,
):
    me = lax.axis_index("expert")
    my_dp = lax.axis_index("dp")
    my_z = lax.div(my_dp, inner)
    my_x = lax.rem(my_dp, inner)
    my_zh = lax.div(my_z, 2)
    my_zl = lax.rem(my_z, 2)
    other_x = 1 - my_x
    partner_dp = my_z * inner + other_x
    mate_dp = flipped(my_z, 1) * inner + my_x
    local, d_model, ff2 = wgu.shape
    ff = ff2 // 2
    part = local // 2
    mine = my_zl * part
    tokens = rows_r.shape[3]
    split = tokens // 2
    cap = slot_gate.shape[2]
    rows = parts.shape[4]

    inputs = [
        pltpu.make_async_copy(src, dst, in_sem.at[i])
        for i, (src, dst) in enumerate(
            ((ids_h, ids_r.at[0, 0]), (gates_h, gates_r.at[0, 0]), (tok_h, rows_r.at[0, 0, 0]), (cot_h, rows_r.at[1, 0, 0]))
        )
    ]
    for c in inputs:
        c.start()
    loads = [
        pltpu.make_async_copy(wg_h, wgu.at[:, :, pl.ds(0, ff)], w_sem.at[0]),
        pltpu.make_async_copy(wu_h, wgu.at[:, :, pl.ds(ff, ff)], w_sem.at[1]),
        pltpu.make_async_copy(wd_h, wd, w_sem.at[2]),
    ]

    barrier = pltpu.get_barrier_semaphore()
    for k in range(1, n):
        pl.semaphore_signal(barrier, inc=1, device_id={"expert": flipped(me, k)})
    for k in range(1, n):
        pl.semaphore_signal(barrier, inc=1, device_id={"dp": mate_dp, "expert": flipped(me, k)})
    pl.semaphore_signal(barrier, inc=1, device_id={"dp": partner_dp})
    for k in range(1, outer):
        pl.semaphore_signal(barrier, inc=1, device_id={"dp": flipped(my_z, k) * inner + my_x})
    pl.semaphore_wait(barrier, 2 * (n - 1) + 1 + (outer - 1))

    def send(src, dst, s, r, **where):
        return pltpu.make_async_remote_copy(src_ref=src, dst_ref=dst, send_sem=s, recv_sem=r, device_id=where)

    def meta_copies(s, k):
        where = {"expert": flipped(me, k)} if k else {}
        if s:
            where["dp"] = mate_dp
        return [
            send(a.at[0, 0], a.at[s, k], ms_sem.at[i, s, k], mr_sem.at[i, s, k], **where)
            for i, a in enumerate((ids_r, gates_r))
        ]

    def row_copies(t, s, k, halves=(0, 1)):
        sems = lambda h: (gs_sem.at[t, s, k, h], gr_sem.at[t, s, k, h])
        landed = rows_r.at[t, s, k]
        if s == 0:
            if k % 2 and k > 1:
                return [send(rows_r.at[t, 0, k - 1], landed, *sems(0), expert=flipped(me, 1))]
            return [send(rows_r.at[t, 0, 0], landed, *sems(0), expert=flipped(me, k))]
        if k == 0:
            return [send(rows_r.at[t, 0, 0], landed, *sems(0), dp=mate_dp)]
        if k % 2:
            return [send(rows_r.at[t, 1, k - 1], landed, *sems(0), expert=flipped(me, 1))]
        span = (pl.ds(0, split), pl.ds(split, tokens - split))
        src = (rows_r.at[t, 0, k], rows_r.at[t, 1, 0])
        where = ({"dp": mate_dp}, {"expert": flipped(me, k)})
        return [send(src[h].at[span[h]], landed.at[span[h]], *sems(h), **where[h]) for h in halves]

    def start(copies):
        for c in copies:
            c.start()

    def landed(copies):
        for c in copies:
            c.wait_recv()

    def left(copies):
        for c in copies:
            c.wait_send()

    for c in inputs:
        c.wait()
    pairs = [(0, k) for k in range(1, n)] + [(1, k) for k in range(n)]
    for s, k in pairs:
        start(meta_copies(s, k))
    direct = [(0, k) for k in range(2, n, 2)] + [(1, 0), (0, 1)]
    for t in range(2):
        for s, k in direct:
            start(row_copies(t, s, k))
    for c in loads:
        c.start()

    above = (
        lax.broadcasted_iota(jnp.int32, (tokens, tokens), 0)
        < lax.broadcasted_iota(jnp.int32, (tokens, tokens), 1)
    )
    before = jnp.where(above, 1.0, 0.0).astype(BF)
    padded = -(-local // 8) * 8

    def route(s, k):
        if s or k:
            landed(meta_copies(s, k))
        iv, gv = ids_r[s, k], gates_r[s, k]
        count, first = (part, me * local + mine) if s else (local, me * local)
        hots, values = (hot1, slot_gate1) if s else (hot, slot_gate)
        expert = lax.broadcasted_iota(jnp.int32, (padded, tokens), 0) + first
        hit = jnp.zeros((padded, tokens), F32)
        gate = jnp.zeros((padded, tokens), F32)
        for c in range(top):
            same = iv[c : c + 1] == expert
            hit = hit + jnp.where(same, 1.0, 0.0)
            gate = gate + jnp.where(same, gv[c : c + 1].astype(F32) * (1.0 / 65536.0), 0.0)
        rank = dot(hit.astype(BF), before)
        rank = jnp.where(hit > 0.5, rank, -1.0)
        slot = lax.broadcasted_iota(jnp.int32, (cap, tokens), 0).astype(F32)
        for i in range(count):
            picked = jnp.where(slot == rank[i : i + 1], 1.0, 0.0)
            hots[k, i * cap : (i + 1) * cap] = picked.astype(BF)
            value = jnp.sum(picked * gate[i : i + 1], axis=1, keepdims=True)
            values[k, i] = jnp.broadcast_to(value, (cap, 128))

    def take(t, s, k):
        got = dot((hot1 if s else hot)[k], rows_r[t, s, k])
        count = part if s else local
        into = ((xs, gs), (xs1, gs1))[s][t]
        for i in range(count):
            value = got[i * cap : (i + 1) * cap]
            if t:
                value = (slot_gate1 if s else slot_gate)[k, i][:, :1] * value
            into[i, k * cap : (k + 1) * cap] = value.astype(BF)

    def x_copy(i, a, k):
        zz = flipped(my_z, k)
        return send(
            parts.at[other_x, i, a, zz], x_r.at[i, a, zz], xs_sem.at[i, a, k], xr_sem.at[i, a, k], dp=partner_dp
        )

    def z_copy(k, i, a):
        there = flipped(my_z, k)
        return send(
            z_s.at[i, a, there], z_r.at[k, i, a], zs_sem.at[k, i, a], zr_sem.at[k, i, a],
            dp=there * inner + my_x,
        )

    def put(i, a, value):
        for zz in range(outer):
            for xx in range(inner):
                at = (zz * inner + xx) * rows
                parts[xx, i, a, zz] = value[at : at + rows].astype(BF)
        for k in range(outer - 1, 1, -1):
            x_copy(i, a, k).start()

    def grads(hidden_grad, p, into, e):
        pre_gate, pre_up = p[:, :ff], p[:, ff:]
        sig = jax.nn.sigmoid(pre_gate)
        into[e, :, ff:] = (hidden_grad * (pre_gate * sig)).astype(BF)
        into[e, :, :ff] = (hidden_grad * pre_up * sig * (1.0 + pre_gate * (1.0 - sig))).astype(BF)

    def forward(e, carry):
        p = dot(xs[e], wgu[e])
        pre[e] = p
        pre_gate, pre_up = p[:, :ff], p[:, ff:]
        hidden = (pre_gate * jax.nn.sigmoid(pre_gate) * pre_up).astype(BF)
        hs[e] = hidden
        o = dot(hidden, wd[e], 1, 1).astype(BF).astype(F32)
        for k in range(n):
            ys[k, e] = (slot_gate[k, e][:, :1] * o[k * cap : (k + 1) * cap]).astype(BF)
        return carry

    def backward(e, carry):
        grads(dot(gs[e], wd[e]), pre[e], gu, e)
        back = dot(gu[e], wgu[e], 1, 1).astype(BF)
        for k in range(n):
            ds[k, e] = back[k * cap : (k + 1) * cap]
        return carry

    def forward_pair(i, carry):
        p = dot(xs1[i], wgu[mine + i])
        pre[mine + i] = p
        pre_gate, pre_up = p[:, :ff], p[:, ff:]
        hs1[i] = (pre_gate * jax.nn.sigmoid(pre_gate) * pre_up).astype(BF)
        return carry

    def y_copy(j, k):
        return send(rows_r.at[j, 0, k], y_r.at[j, k], ys_sem.at[j, k], yr_sem.at[j, k], expert=flipped(me, k))

    def spread(j, k):
        src = (ys, ds)[j]
        return dot(hot[k], src[k].reshape(local * cap, d_model), 0, 0)

    def back_out(j):
        for k in range(n - 1, 0, -1):
            if k % 2 == 0:
                left(row_copies(j, 0, k + 1) + row_copies(j, 1, k, (0,)))
            rows_r[j, 0, k] = spread(j, k).astype(BF)
            y_copy(j, k).start()

    def act_copy(j):
        return pltpu.make_async_copy(act_s.at[j], act_o.at[j], out_sem.at[j])

    def grad_copy(a, i):
        return pltpu.make_async_copy(grad_s.at[a, i], grad_o.at[a, i], out_sem.at[2 + a * local + i])

    def returned(j):
        total = spread(j, 0)
        for k in range(1, n):
            y_copy(j, k).wait_recv()
            total = total + y_r[j, k].astype(F32)
        act_s[j] = total.astype(BF)
        act_copy(j).start()

    def x_stage(i, a, k):
        zz = flipped(my_z, k)
        x_copy(i, a, k).wait_recv()
        z_s[i, a, zz] = (parts[my_x, i, a, zz].astype(F32) + x_r[i, a, zz].astype(F32)).astype(BF)
        if k:
            z_copy(k, i, a).start()

    def finish(i, a):
        for first, e in ((0, mine + i), (1, part - mine + i)):
            total = 0.0
            for k in range(first, outer, 2):
                if k:
                    z_copy(k, i, a).wait_recv()
                total = total + (z_r[k, i, a] if k else z_s[i, a, my_z]).astype(F32)
            grad_s[a, e] = total * scale
            grad_copy(a, e).start()

    even = range(2, n, 2)

    def relay(t):
        for k in even:
            landed(row_copies(t, 0, k))
            start(row_copies(t, 0, k + 1))
            start(row_copies(t, 1, k, (0,)))
        landed(row_copies(t, 1, 0))
        for k in even:
            start(row_copies(t, 1, k, (1,)))
        start(row_copies(t, 1, 1))
        for k in even:
            take(t, 0, k)
        take(t, 1, 0)
        for k in even:
            landed(row_copies(t, 0, k + 1))
            take(t, 0, k + 1)
        landed(row_copies(t, 1, 1))
        take(t, 1, 1)

    def far_first(t):
        for k in even:
            landed(row_copies(t, 1, k))
            start(row_copies(t, 1, k + 1))
            take(t, 1, k)

    def far_last(t):
        for k in even:
            landed(row_copies(t, 1, k + 1))
            take(t, 1, k + 1)

    route(0, 0)
    for t in range(2):
        take(t, 0, 0)
    for s, k in pairs:
        route(s, k)
    for t in range(2):
        landed(row_copies(t, 0, 1))
        take(t, 0, 1)
    relay(0)
    for c in loads:
        c.wait()
    lax.fori_loop(0, local, forward, 0)
    relay(1)
    lax.fori_loop(mine, mine + 1, backward, 0)
    far_first(0)
    lax.fori_loop(mine + 1, mine + part, backward, 0)
    back_out(0)
    far_last(0)
    lax.fori_loop(0, part, forward_pair, 0)
    far_first(1)
    lax.fori_loop(part - mine, local - mine, backward, 0)
    far_last(1)

    order = (2, 0, 1)
    for i in range(part):
        e = mine + i
        put(i, 2, dot(gs[e], hs[e], 0, 0) + dot(gs1[i], hs1[i], 0, 0))
        grads(dot(gs1[i], wd[e]), pre[e], gu1, i)
        if i == part - 1:
            for k in range(outer - 1, 1, -1):
                x_stage(0, 2, k)
        both = dot(xs[e], gu[e], 0, 0) + dot(xs1[i], gu1[i], 0, 0)
        put(i, 0, both[:, :ff])
        put(i, 1, both[:, ff:])

    for k in (1, 0):
        for i in range(part):
            for a in order:
                x_copy(i, a, k).start()
    back_out(1)
    for i in range(part):
        for a in order:
            if i or a != 2:
                for k in range(outer - 1, 1, -1):
                    x_stage(i, a, k)
    returned(0)
    for i in range(part):
        for a in order:
            x_stage(i, a, 1)
    returned(1)
    for i in range(part):
        for a in order:
            x_stage(i, a, 0)
            finish(i, a)

    for s, k in pairs:
        left(meta_copies(s, k))
        for t in range(2):
            if s or k < 2 or k % 2 == 0:
                left(row_copies(t, s, k, (1,)))
    for j in range(2):
        for k in range(1, n):
            y_copy(j, k).wait_send()

    def drain(i, carry):
        for a in range(3):
            for k in range(outer):
                x_copy(i, a, k).wait_send()
                if k:
                    z_copy(k, i, a).wait_send()
        return carry

    lax.fori_loop(0, part, drain, 0)
    for j in range(2):
        act_copy(j).wait()
    for a in range(3):
        for e in range(local):
            grad_copy(a, e).wait()


def write(act, grad, out_o, din_o, gg_o, gu_o, gd_o, sem):
    srcs = (act.at[0], act.at[1], grad.at[0], grad.at[1], grad.at[2])
    copies = [
        pltpu.make_async_copy(src, dst, sem.at[i]) for i, (src, dst) in enumerate(zip(srcs, (out_o, din_o, gg_o, gu_o, gd_o)))
    ]
    for c in copies:
        c.start()
    for c in copies:
        c.wait()


def padded_bytes(ref):
    size = jnp.dtype(ref.dtype).itemsize
    *lead, high, low = ref.shape
    total = size * (-(-high * size // 32) * 32 // size) * (-(-low // 128) * 128)
    for extent in lead:
        total *= extent
    return total


def shards(tokens, expert_ids, gate_fixed, cotangent, w_gate, w_up, w_down):
    n = lax.axis_size("expert")
    replicas = lax.axis_size("dp")
    inner = 2
    outer = replicas // inner
    local, d_model, ff = w_gate.shape
    count, top = expert_ids.shape
    cap = count * top * 2 // (local * n)
    rows = d_model // replicas
    part = local // 2
    scale = float(count * n * replicas * top // (local * n)) ** (-0.5)
    hbm = pl.BlockSpec(memory_space=pl.ANY)
    dma = pltpu.SemaphoreType.DMA
    slots = n * cap
    buffers = [
        pltpu.VMEM((2, count, d_model), BF),
        pltpu.VMEM((3, local, rows, ff), F32),
        pltpu.VMEM((local, d_model, 2 * ff), BF),
        pltpu.VMEM((local, d_model, ff), BF),
        pltpu.VMEM((2, n, top, count), jnp.int32),
        pltpu.VMEM((2, n, top, count), jnp.int32),
        pltpu.VMEM((2, 2, n, count, d_model), BF),
        pltpu.VMEM((n, local * cap, count), BF),
        pltpu.VMEM((n, part * cap, count), BF),
        pltpu.VMEM((n, local, cap, 128), F32),
        pltpu.VMEM((n, part, cap, 128), F32),
        pltpu.VMEM((local, slots, d_model), BF),
        pltpu.VMEM((local, slots, d_model), BF),
        pltpu.VMEM((part, slots, d_model), BF),
        pltpu.VMEM((part, slots, d_model), BF),
        pltpu.VMEM((local, slots, ff), BF),
        pltpu.VMEM((part, slots, ff), BF),
        pltpu.VMEM((local, slots, 2 * ff), F32),
        pltpu.VMEM((local, slots, 2 * ff), BF),
        pltpu.VMEM((part, slots, 2 * ff), BF),
        pltpu.VMEM((n, local, cap, d_model), BF),
        pltpu.VMEM((n, local, cap, d_model), BF),
        pltpu.VMEM((2, n, count, d_model), BF),
        pltpu.VMEM((inner, part, 3, outer, rows, ff), BF),
        pltpu.VMEM((part, 3, outer, rows, ff), BF),
        pltpu.VMEM((part, 3, outer, rows, ff), BF),
        pltpu.VMEM((outer, part, 3, rows, ff), BF),
    ]
    args = (expert_ids.T, gate_fixed.T, tokens, cotangent, w_gate, w_up, w_down)
    act, grad = pl.pallas_call(
        functools.partial(kernel, n, inner, outer, top, scale),
        out_shape=(
            jax.ShapeDtypeStruct((2, count, d_model), BF),
            jax.ShapeDtypeStruct((3, local, rows, ff), F32),
        ),
        in_specs=[hbm] * 7,
        out_specs=(hbm,) * 2,
        scratch_shapes=buffers + [
            dma((3,)), dma((4,)), dma((2 + 3 * local,)),
            dma((2, 2, n)), dma((2, 2, n)),
            dma((2, 2, n, 2)), dma((2, 2, n, 2)),
            dma((2, n)), dma((2, n)),
            dma((part, 3, outer)), dma((part, 3, outer)),
            dma((outer, part, 3)), dma((outer, part, 3)),
        ],
        compiler_params=pltpu.CompilerParams(
            collective_id=0,
            has_side_effects=True,
            vmem_limit_bytes=min(sum(map(padded_bytes, buffers)) + MARGIN, 62 * 1024 * 1024),
        ),
    )(*(pltpu.with_memory_space_constraint(v, pltpu.HBM) for v in args))
    act_block = jax.ShapeDtypeStruct((count, d_model), BF)
    grad_block = jax.ShapeDtypeStruct((local, rows, ff), F32)
    return pl.pallas_call(
        write,
        out_shape=(act_block, act_block, grad_block, grad_block, grad_block),
        in_specs=[hbm] * 2,
        out_specs=(hbm,) * 5,
        scratch_shapes=[dma((5,))],
        compiler_params=pltpu.CompilerParams(vmem_limit_bytes=1024 * 1024),
    )(act, grad)


def solution(mesh):
    return jax.shard_map(
        shards,
        mesh=mesh,
        in_specs=(P(("dp", "expert"), None),) * 4 + (P("expert", None, None),) * 3,
        out_specs=(P(("dp", "expert"), None),) * 2 + (P("expert", "dp", None),) * 3,
        check_vma=False,
    )
```

```python
import functools

import jax
import jax.numpy as jnp
from jax import lax
from jax.experimental import pallas as pl
from jax.experimental.pallas import tpu as pltpu
from jax.sharding import PartitionSpec as P

BF = jnp.bfloat16
F32 = jnp.float32
MARGIN = 6 * 1024 * 1024


def dot(a, b, ca=1, cb=0):
    return lax.dot_general(a, b, (((ca,), (cb,)), ((), ())), preferred_element_type=F32)


def flipped(me, k):
    out, bit = me, 1
    while bit <= k:
        if k & bit:
            out = out + bit * (1 - 2 * lax.rem(lax.div(me, bit), 2))
        bit *= 2
    return out


def kernel(
    n, inner, outer, top, scale,
    ids_h, gates_h, tok_h, cot_h, wg_h, wu_h, wd_h,
    act_o, grad_o,
    act_s, grad_s, wgu, wd, meta_r, rows_r, hot, hot1, slot_gate, slot_gate1,
    xs, gs, xs1, gs1, hs, hs1, pre, gu, gu1, ys, ds, y_r, parts, x_r, z_s, z_r,
    w_sem, in_sem, out_sem, ms_sem, mr_sem, gs_sem, gr_sem, ys_sem, yr_sem, xs_sem, xr_sem, zs_sem, zr_sem,
):
    me = lax.axis_index("expert")
    my_dp = lax.axis_index("dp")
    my_z = lax.div(my_dp, inner)
    my_x = lax.rem(my_dp, inner)
    my_zh = lax.div(my_z, 2)
    my_zl = lax.rem(my_z, 2)
    other_x = 1 - my_x
    partner_dp = my_z * inner + other_x
    mate_dp = flipped(my_z, 1) * inner + my_x
    local, d_model, ff2 = wgu.shape
    ff = ff2 // 2
    part = local // 2
    mine = my_zl * part
    tokens = rows_r.shape[3]
    split = tokens // 2
    cap = slot_gate.shape[2]
    rows = parts.shape[4]

    inputs = [
        pltpu.make_async_copy(src, dst, in_sem.at[i])
        for i, (src, dst) in enumerate(
            (
                (ids_h, meta_r.at[0, pl.ds(0, top)]),
                (gates_h, meta_r.at[0, pl.ds(top, top)]),
                (tok_h, rows_r.at[0, 0, 0]),
                (cot_h, rows_r.at[1, 0, 0]),
            )
        )
    ]
    for c in inputs:
        c.start()
    loads = [
        pltpu.make_async_copy(wg_h, wgu.at[:, :, pl.ds(0, ff)], w_sem.at[0]),
        pltpu.make_async_copy(wu_h, wgu.at[:, :, pl.ds(ff, ff)], w_sem.at[1]),
        pltpu.make_async_copy(wd_h, wd, w_sem.at[2]),
    ]

    barrier = pltpu.get_barrier_semaphore()
    for k in range(1, n):
        pl.semaphore_signal(barrier, inc=1, device_id={"expert": flipped(me, k)})
    for k in range(1, n):
        pl.semaphore_signal(barrier, inc=1, device_id={"dp": mate_dp, "expert": flipped(me, k)})
    pl.semaphore_signal(barrier, inc=1, device_id={"dp": partner_dp})
    for k in range(1, outer):
        pl.semaphore_signal(barrier, inc=1, device_id={"dp": flipped(my_z, k) * inner + my_x})
    pl.semaphore_wait(barrier, 2 * (n - 1) + 1 + (outer - 1))

    def send(src, dst, s, r, **where):
        return pltpu.make_async_remote_copy(src_ref=src, dst_ref=dst, send_sem=s, recv_sem=r, device_id=where)

    def meta_copy(s, k):
        where = {"expert": flipped(me, k)} if k else {}
        if s:
            where["dp"] = mate_dp
        return send(meta_r.at[0], meta_r.at[s * n + k], ms_sem.at[0], mr_sem.at[0], **where)

    others = pl.ds(1, 2 * n - 1)
    all_meta = send(meta_r.at[others], meta_r.at[others], ms_sem.at[0], mr_sem.at[0], dp=mate_dp)

    def spot(s, k, h):
        return 2 * n - 1 + k // 2 - 1 if h else s * n + k - 1

    def row_copies(t, s, k, halves=(0, 1)):
        sems = lambda h: (gs_sem.at[t, spot(s, k, h)], gr_sem.at[t, spot(s, k, h)])
        landed = rows_r.at[t, s, k]
        if s == 0:
            if k % 2 and k > 1:
                return [send(rows_r.at[t, 0, k - 1], landed, *sems(0), expert=flipped(me, 1))]
            return [send(rows_r.at[t, 0, 0], landed, *sems(0), expert=flipped(me, k))]
        if k == 0:
            return [send(rows_r.at[t, 0, 0], landed, *sems(0), dp=mate_dp)]
        if k % 2:
            return [send(rows_r.at[t, 1, k - 1], landed, *sems(0), expert=flipped(me, 1))]
        span = (pl.ds(0, split), pl.ds(split, tokens - split))
        src = (rows_r.at[t, 0, k], rows_r.at[t, 1, 0])
        where = ({"dp": mate_dp}, {"expert": flipped(me, k)})
        return [send(src[h].at[span[h]], landed.at[span[h]], *sems(h), **where[h]) for h in halves]

    def start(copies):
        for c in copies:
            c.start()

    def landed(copies):
        for c in copies:
            c.wait_recv()

    def left(copies):
        for c in copies:
            c.wait_send()

    for c in inputs:
        c.wait()
    pairs = [(0, k) for k in range(1, n)] + [(1, k) for k in range(n)]
    for s, k in pairs:
        meta_copy(s, k).start()
    direct = [(0, k) for k in range(2, n, 2)] + [(1, 0), (0, 1)]
    for t in range(2):
        for s, k in direct:
            start(row_copies(t, s, k))
    for c in loads:
        c.start()

    above = (
        lax.broadcasted_iota(jnp.int32, (tokens, tokens), 0)
        < lax.broadcasted_iota(jnp.int32, (tokens, tokens), 1)
    )
    before = jnp.where(above, 1.0, 0.0).astype(BF)
    padded = -(-local // 8) * 8

    def route(s, k):
        mv = meta_r[s * n + k]
        count, first = (part, me * local + mine) if s else (local, me * local)
        hots, values = (hot1, slot_gate1) if s else (hot, slot_gate)
        expert = lax.broadcasted_iota(jnp.int32, (padded, tokens), 0) + first
        hit = jnp.zeros((padded, tokens), F32)
        gate = jnp.zeros((padded, tokens), F32)
        for c in range(top):
            same = mv[c : c + 1] == expert
            hit = hit + jnp.where(same, 1.0, 0.0)
            gate = gate + jnp.where(same, mv[top + c : top + c + 1].astype(F32) * (1.0 / 65536.0), 0.0)
        rank = dot(hit.astype(BF), before)
        rank = jnp.where(hit > 0.5, rank, -1.0)
        slot = lax.broadcasted_iota(jnp.int32, (cap, tokens), 0).astype(F32)
        for i in range(count):
            picked = jnp.where(slot == rank[i : i + 1], 1.0, 0.0)
            hots[k, i * cap : (i + 1) * cap] = picked.astype(BF)
            value = jnp.sum(picked * gate[i : i + 1], axis=1, keepdims=True)
            values[k, i] = jnp.broadcast_to(value, (cap, 128))

    def take(t, s, k):
        got = dot((hot1 if s else hot)[k], rows_r[t, s, k])
        count = part if s else local
        into = ((xs, gs), (xs1, gs1))[s][t]
        for i in range(count):
            value = got[i * cap : (i + 1) * cap]
            if t:
                value = (slot_gate1 if s else slot_gate)[k, i][:, :1] * value
            into[i, k * cap : (k + 1) * cap] = value.astype(BF)

    def x_copy(i, a, k):
        zz = flipped(my_z, k)
        return send(
            parts.at[other_x, i, a, zz], x_r.at[i, a, zz], xs_sem.at[0], xr_sem.at[i, a, k], dp=partner_dp
        )

    def z_copy(k, i, a):
        there = flipped(my_z, k)
        return send(
            z_s.at[i, a, there], z_r.at[i, a, k], zs_sem.at[0], zr_sem.at[i, a],
            dp=there * inner + my_x,
        )

    def put(i, a, half, value):
        for zz in range(outer // 2):
            for xx in range(inner):
                at = (zz * inner + xx) * rows
                parts[xx, i, a, half * (outer // 2) + zz] = value[at : at + rows].astype(BF)

    def grads(hidden_grad, p, into, e):
        pre_gate, pre_up = p[:, :ff], p[:, ff:]
        sig = jax.nn.sigmoid(pre_gate)
        into[e, :, ff:] = (hidden_grad * (pre_gate * sig)).astype(BF)
        into[e, :, :ff] = (hidden_grad * pre_up * sig * (1.0 + pre_gate * (1.0 - sig))).astype(BF)

    def forward(e, carry):
        p = dot(xs[e], wgu[e])
        pre[e] = p
        pre_gate, pre_up = p[:, :ff], p[:, ff:]
        hidden = (pre_gate * jax.nn.sigmoid(pre_gate) * pre_up).astype(BF)
        hs[e] = hidden
        o = dot(hidden, wd[e], 1, 1).astype(BF).astype(F32)
        for k in range(n):
            ys[k, e] = (slot_gate[k, e][:, :1] * o[k * cap : (k + 1) * cap]).astype(BF)
        return carry

    def backward(e, carry):
        grads(dot(gs[e], wd[e]), pre[e], gu, e)
        back = dot(gu[e], wgu[e], 1, 1).astype(BF)
        for k in range(n):
            ds[k, e] = back[k * cap : (k + 1) * cap]
        return carry

    def forward_pair(i, carry):
        p = dot(xs1[i], wgu[mine + i])
        pre[mine + i] = p
        pre_gate, pre_up = p[:, :ff], p[:, ff:]
        hs1[i] = (pre_gate * jax.nn.sigmoid(pre_gate) * pre_up).astype(BF)
        return carry

    def y_copy(j, k):
        return send(rows_r.at[j, 0, k], y_r.at[j, k], ys_sem.at[j], yr_sem.at[j], expert=flipped(me, k))

    def y_all(j):
        away = pl.ds(1, n - 1)
        return send(y_r.at[j, away], y_r.at[j, away], ys_sem.at[j], yr_sem.at[j], dp=mate_dp)

    def spread(j, k):
        src = (ys, ds)[j]
        return dot(hot[k], src[k].reshape(local * cap, d_model), 0, 0)

    def back_out(j):
        for k in range(n - 1, 0, -1):
            if k % 2 == 0:
                left(row_copies(j, 0, k + 1) + row_copies(j, 1, k, (0,)))
            rows_r[j, 0, k] = spread(j, k).astype(BF)
            y_copy(j, k).start()

    def act_copy(j):
        return pltpu.make_async_copy(act_s.at[j], act_o.at[j], out_sem.at[0])

    def grad_copy(a, i):
        return pltpu.make_async_copy(grad_s.at[a, i], grad_o.at[a, i], out_sem.at[1])

    def returned(j):
        total = spread(j, 0)
        y_all(j).wait_recv()
        for k in range(1, n):
            total = total + y_r[j, k].astype(F32)
        act_s[j] = total.astype(BF)
        act_copy(j).start()

    def x_stage(i, a, k):
        zz = flipped(my_z, k)
        x_copy(i, a, k).wait_recv()
        z_s[i, a, zz] = (parts[my_x, i, a, zz].astype(F32) + x_r[i, a, zz].astype(F32)).astype(BF)
        if k:
            z_copy(k, i, a).start()

    def finish(i, a):
        far_z = pl.ds(1, outer - 1)
        send(z_r.at[i, a, far_z], z_r.at[i, a, far_z], zs_sem.at[0], zr_sem.at[i, a], dp=mate_dp).wait_recv()
        for first, e in ((0, mine + i), (1, part - mine + i)):
            total = 0.0
            for k in range(first, outer, 2):
                total = total + (z_r[i, a, k] if k else z_s[i, a, my_z]).astype(F32)
            grad_s[a, e] = total * scale
            grad_copy(a, e).start()

    even = range(2, n, 2)

    def relay(t):
        for k in even:
            landed(row_copies(t, 0, k))
            start(row_copies(t, 0, k + 1))
            start(row_copies(t, 1, k, (0,)))
        landed(row_copies(t, 1, 0))
        for k in even:
            start(row_copies(t, 1, k, (1,)))
        start(row_copies(t, 1, 1))
        for k in even:
            take(t, 0, k)
        take(t, 1, 0)
        for k in even:
            landed(row_copies(t, 0, k + 1))
            take(t, 0, k + 1)
        landed(row_copies(t, 1, 1))
        take(t, 1, 1)

    def far_first(t):
        for k in even:
            landed(row_copies(t, 1, k))
            start(row_copies(t, 1, k + 1))
            take(t, 1, k)

    def far_last(t):
        for k in even:
            landed(row_copies(t, 1, k + 1))
            take(t, 1, k + 1)

    route(0, 0)
    for t in range(2):
        take(t, 0, 0)
    all_meta.wait_recv()
    for s, k in pairs:
        route(s, k)
    for t in range(2):
        landed(row_copies(t, 0, 1))
        take(t, 0, 1)
    relay(0)
    for c in loads:
        c.wait()
    lax.fori_loop(0, local, forward, 0)
    relay(1)
    lax.fori_loop(mine, mine + 1, backward, 0)
    far_first(0)
    lax.fori_loop(mine + 1, mine + part, backward, 0)
    back_out(0)
    far_last(0)
    lax.fori_loop(0, part, forward_pair, 0)
    far_first(1)
    lax.fori_loop(part - mine, local - mine, backward, 0)
    cut = d_model // 2
    near = lax.div(my_z, outer // 2)

    def columns(ref, i, half):
        return ref[i, :, pl.ds(pl.multiple_of(half * cut, cut), cut)]

    def own_down(i, half):
        return dot(columns(gs, mine + i, half), hs[mine + i], 0, 0)

    def put_down(i, half, seed):
        put(i, 2, half, seed + dot(columns(gs1, i, half), hs1[i], 0, 0))

    def put_both(i, half):
        both = dot(columns(xs, mine + i, half), gu[mine + i], 0, 0) + dot(columns(xs1, i, half), gu1[i], 0, 0)
        put(i, 0, half, both[:, :ff])
        put(i, 1, half, both[:, ff:])

    def x_start(i, a, ks):
        for k in ks:
            x_copy(i, a, k).start()

    order = (2, 0, 1)
    chunks = [(i, a) for i in range(part) for a in order]
    far_ks = range(outer - 1, outer // 2 - 1, -1)
    near_ks = range(outer // 2 - 1, 0, -1)

    seed = own_down(0, 1 - near)
    far_last(1)
    for i in range(part):
        put_down(i, 1 - near, seed if i == 0 else own_down(i, 1 - near))
        x_start(i, 2, far_ks)
        grads(dot(gs1[i], wd[mine + i]), pre[mine + i], gu1, i)
        if i == part - 1:
            for k in far_ks:
                x_stage(0, 2, k)
        put_both(i, 1 - near)
        x_start(i, 0, far_ks)
        x_start(i, 1, far_ks)
    for i in range(part):
        put_down(i, near, own_down(i, near))
        put_both(i, near)
        for a in order:
            x_start(i, a, near_ks)
        for k in far_ks:
            x_stage(*chunks[1 + i], k)
    for i, a in chunks:
        x_start(i, a, (0,))
    back_out(1)
    for i, a in chunks[1 + part :]:
        for k in far_ks:
            x_stage(i, a, k)
    returned(0)
    for i, a in chunks:
        for k in near_ks:
            x_stage(i, a, k)
    returned(1)
    for i, a in chunks:
        x_stage(i, a, 0)
        finish(i, a)

    all_meta.wait_send()
    for s, k in pairs:
        for t in range(2):
            if s or k < 2 or k % 2 == 0:
                left(row_copies(t, s, k, (1,)))
    for j in range(2):
        y_all(j).wait_send()
    send(parts.at[other_x], x_r, xs_sem.at[0], xr_sem.at[0, 0, 0], dp=partner_dp).wait_send()
    sent = z_r.at[:, :, pl.ds(1, outer - 1)]
    send(sent, sent, zs_sem.at[0], zr_sem.at[0, 0], dp=mate_dp).wait_send()
    pltpu.make_async_copy(act_s, act_o, out_sem.at[0]).wait()
    pltpu.make_async_copy(grad_s, grad_o, out_sem.at[1]).wait()


def write(act, grad, out_o, din_o, gg_o, gu_o, gd_o, sem):
    srcs = (act.at[0], act.at[1], grad.at[0], grad.at[1], grad.at[2])
    copies = [
        pltpu.make_async_copy(src, dst, sem.at[i]) for i, (src, dst) in enumerate(zip(srcs, (out_o, din_o, gg_o, gu_o, gd_o)))
    ]
    for c in copies:
        c.start()
    for c in copies:
        c.wait()


def padded_bytes(ref):
    size = jnp.dtype(ref.dtype).itemsize
    *lead, high, low = ref.shape
    total = size * (-(-high * size // 32) * 32 // size) * (-(-low // 128) * 128)
    for extent in lead:
        total *= extent
    return total


def shards(tokens, expert_ids, gate_fixed, cotangent, w_gate, w_up, w_down):
    n = lax.axis_size("expert")
    replicas = lax.axis_size("dp")
    inner = 2
    outer = replicas // inner
    local, d_model, ff = w_gate.shape
    count, top = expert_ids.shape
    cap = count * top * 2 // (local * n)
    rows = d_model // replicas
    part = local // 2
    scale = float(count * n * replicas * top // (local * n)) ** (-0.5)
    hbm = pl.BlockSpec(memory_space=pl.ANY)
    dma = pltpu.SemaphoreType.DMA
    slots = n * cap
    buffers = [
        pltpu.VMEM((2, count, d_model), BF),
        pltpu.VMEM((3, local, rows, ff), F32),
        pltpu.VMEM((local, d_model, 2 * ff), BF),
        pltpu.VMEM((local, d_model, ff), BF),
        pltpu.VMEM((2 * n, 2 * top, count), jnp.int32),
        pltpu.VMEM((2, 2, n, count, d_model), BF),
        pltpu.VMEM((n, local * cap, count), BF),
        pltpu.VMEM((n, part * cap, count), BF),
        pltpu.VMEM((n, local, cap, 128), F32),
        pltpu.VMEM((n, part, cap, 128), F32),
        pltpu.VMEM((local, slots, d_model), BF),
        pltpu.VMEM((local, slots, d_model), BF),
        pltpu.VMEM((part, slots, d_model), BF),
        pltpu.VMEM((part, slots, d_model), BF),
        pltpu.VMEM((local, slots, ff), BF),
        pltpu.VMEM((part, slots, ff), BF),
        pltpu.VMEM((local, slots, 2 * ff), F32),
        pltpu.VMEM((local, slots, 2 * ff), BF),
        pltpu.VMEM((part, slots, 2 * ff), BF),
        pltpu.VMEM((n, local, cap, d_model), BF),
        pltpu.VMEM((n, local, cap, d_model), BF),
        pltpu.VMEM((2, n, count, d_model), BF),
        pltpu.VMEM((inner, part, 3, outer, rows, ff), BF),
        pltpu.VMEM((part, 3, outer, rows, ff), BF),
        pltpu.VMEM((part, 3, outer, rows, ff), BF),
        pltpu.VMEM((part, 3, outer, rows, ff), BF),
    ]
    args = (expert_ids.T, gate_fixed.T, tokens, cotangent, w_gate, w_up, w_down)
    act, grad = pl.pallas_call(
        functools.partial(kernel, n, inner, outer, top, scale),
        out_shape=(
            jax.ShapeDtypeStruct((2, count, d_model), BF),
            jax.ShapeDtypeStruct((3, local, rows, ff), F32),
        ),
        in_specs=[hbm] * 7,
        out_specs=(hbm,) * 2,
        scratch_shapes=buffers + [
            dma((3,)), dma((4,)), dma((2,)),
            dma((1,)), dma((1,)),
            dma((2, 2 * n - 1 + n // 2 - 1)), dma((2, 2 * n - 1 + n // 2 - 1)),
            dma((2,)), dma((2,)),
            dma((1,)), dma((part, 3, outer)),
            dma((1,)), dma((part, 3)),
        ],
        compiler_params=pltpu.CompilerParams(
            collective_id=0,
            has_side_effects=True,
            vmem_limit_bytes=min(sum(map(padded_bytes, buffers)) + MARGIN, 62 * 1024 * 1024),
        ),
    )(*(pltpu.with_memory_space_constraint(v, pltpu.HBM) for v in args))
    act_block = jax.ShapeDtypeStruct((count, d_model), BF)
    grad_block = jax.ShapeDtypeStruct((local, rows, ff), F32)
    return pl.pallas_call(
        write,
        out_shape=(act_block, act_block, grad_block, grad_block, grad_block),
        in_specs=[hbm] * 2,
        out_specs=(hbm,) * 5,
        scratch_shapes=[dma((5,))],
        compiler_params=pltpu.CompilerParams(vmem_limit_bytes=1024 * 1024),
    )(act, grad)


def solution(mesh):
    return jax.shard_map(
        shards,
        mesh=mesh,
        in_specs=(P(("dp", "expert"), None),) * 4 + (P("expert", None, None),) * 3,
        out_specs=(P(("dp", "expert"), None),) * 2 + (P("expert", "dp", None),) * 3,
        check_vma=False,
    )
```
